32 devices in a mesh: row: 8 (over z, core), feat: 4 (over y, x).
Axes of the slice: x: 2, y: 2, z: 4, core: 2. Of those that a mesh axis runs over, the one named last changes fastest.
Arguments:
- grads: bfloat16 [64, 16384], P(None, ('row', 'feat')), may hold values from -0.75 to 0.75
- codes: int32 [256, 16384], P('feat', 'row'), may hold values from 0 to 127
- node_ids: int32 [16384], P('row'), may hold values from 0 to 7, as said below
- node_slot: int32 [8], replicated, may hold values from 0 to 7, each once
Outputs:
- owned_hist: float32 [8, 64, 32768], P('row', None, 'feat')
The draws below stay inside these ranges and needn't reach their ends.
Inputs may be any that keep to these rules, and one draw needn't show every extreme that they name: `node_ids`: within each panel of 2048 rows the node ids never fall, every node has at most 512 rows in a panel, and every panel has a node with exactly 512 rows.
All inputs are finite; a program needn't handle non-finite values.
Results may differ from the reference program's by a relative error of at most 0.0028.
Values may be sent and summed in bfloat16 or wider, within the bound.
A program may use at most 64 MiB of HBM per device.

```python
import jax
import jax.numpy as jnp
from jax import lax

OUTPUTS = 64
BINS = 128
FEATURES = 256
PANEL = 2048
PANELS = 8
ROWS = 16384
NODES = 8
CAPACITY = 512


def panel_counts(key):

    def counts_of(subkey):
        first_key, second_key = jax.random.split(subkey)
        chosen = jax.random.randint(first_key, (), 0, NODES)
        weights = jax.random.randint(second_key, (NODES,), 2, 4)
        positions = jnp.arange(NODES, dtype=jnp.int32)
        weights = jnp.where(positions == chosen, 0, weights)
        remaining = PANEL - CAPACITY
        shares = weights * remaining // jnp.sum(weights)
        leftover = remaining - jnp.sum(shares)
        ranking = positions - (positions > chosen).astype(jnp.int32)
        extra = jnp.where((positions != chosen) & (ranking < leftover), 1, 0)
        shares = shares + extra
        return jnp.where(positions == chosen, CAPACITY, shares).astype(jnp.int32)
    subkeys = jax.random.split(jax.random.fold_in(key, 7), PANELS)
    return jax.vmap(counts_of)(subkeys)


def draw_node_ids(key, part):
    counts = panel_counts(key)
    ends = jnp.cumsum(counts, axis=1)
    positions = jnp.arange(PANEL, dtype=jnp.int32)
    below = (positions[None, :, None] >= ends[:, None, :]).astype(jnp.int32)
    return jnp.sum(below, axis=2).astype(jnp.int32).reshape(ROWS)


def plant(values, rng, smallest, top_value):
    longest = values.shape.index(max(values.shape))
    spots = []
    for shift in (0, 1):
        where = [jax.random.randint(jax.random.fold_in(rng, axis), (), 0, length) for axis, length in enumerate(values.shape)]
        where[longest] = (where[longest] + shift) % values.shape[longest]
        spots.append(tuple(where))
    return values.at[spots[0]].set(smallest).at[spots[1]].set(top_value)


def level_of(rng, dims, cuts, low, high):
    gain = 1.0
    for position, parts in cuts:
        draws = jax.random.uniform(jax.random.fold_in(jax.random.fold_in(rng, 6), position), (parts,), jnp.float32, low / len(cuts), high / len(cuts))
        gain = gain * jnp.repeat(jnp.exp(draws), dims[position] // parts).reshape((-1,) + (1,) * (len(dims) - 1 - position))
    return gain


def centred(rng, shape, width, bound, shards=(), kind=jnp.bfloat16):
    values = jax.random.normal(rng, shape, jnp.float32) * width
    if len(shards) > 0:
        values = level_of(rng, shape, shards, -0.22, 0.18) * values
    return jnp.clip(values, min=-bound, max=bound).astype(kind)


def setup_inputs(seed: int = 0) -> dict:
    streams_of = jax.random.split(jax.random.key(seed), 5)
    return {
        "grads": centred(streams_of[0], (OUTPUTS, ROWS), 0.125, 0.75, ((1, 32),)),
        "codes": plant(jax.random.randint(streams_of[1], (FEATURES, ROWS), 0, BINS), jax.random.fold_in(streams_of[1], 1), 0, BINS - 1).astype(jnp.int32),
        "node_ids": draw_node_ids(jax.random.fold_in(streams_of[4], 71), 0),
        "node_slot": jax.random.permutation(streams_of[3], NODES).astype(jnp.int32),
    }


def reference(grads, codes, node_ids, node_slot):
    panels = PANELS
    length = grads.shape[1] // panels
    by_panel = grads.reshape(OUTPUTS, panels, length).transpose(1, 2, 0)
    panel_codes = codes.reshape(FEATURES, panels, length).transpose(1, 0, 2)
    panel_ids = node_ids.reshape(panels, length)

    def add_panel(totals, pieces):
        grad_rows, code_rows, id_rows = pieces
        values = grad_rows.astype(jnp.float32)

        def one_feature(feature_codes):
            segment = id_rows * BINS + feature_codes
            return jax.ops.segment_sum(values, segment, num_segments=NODES * BINS)

        partial_sums = lax.map(one_feature, code_rows)
        rounded = lax.optimization_barrier(partial_sums.astype(jnp.bfloat16))
        return totals + rounded.astype(jnp.float32), None

    start_value = jnp.zeros((FEATURES, NODES * BINS, OUTPUTS), jnp.float32)
    totals = lax.scan(add_panel, start_value, (by_panel, panel_codes, panel_ids))[0]
    histogram = totals.reshape(FEATURES, NODES, BINS, OUTPUTS).transpose(1, 3, 0, 2)
    histogram = histogram.reshape(NODES, OUTPUTS, FEATURES * BINS)
    return histogram[node_slot]
```

```python
import functools

import jax
import jax.numpy as jnp
from jax import lax
from jax.experimental import pallas as pl
from jax.experimental.pallas import tpu as pltpu
from jax.sharding import PartitionSpec as P

BINS = 128
LANES = 128
OUTSIDE = 255.0
GROUP = 4
CHUNK = 20


def pack_kernel(starts, nodes, ids_ref, codes_ref, grads_ref, out_ref):
    slots, _, span = out_ref.shape
    features = codes_ref.shape[0]
    for j in range(slots):
        start = pl.multiple_of(starts[j], LANES)
        window = pl.ds(start, span)
        inside = ids_ref[:, window] == nodes[j]
        codes = codes_ref[:, window].astype(jnp.float32)
        codes = jnp.where(jnp.broadcast_to(inside, codes.shape), codes, OUTSIDE)
        out_ref[j, :features, :] = codes.astype(jnp.bfloat16)
        out_ref[j, features:, :] = grads_ref[:, window]


def pack_windows(starts, nodes, ids, codes, grads, span):
    slots = starts.shape[0]
    rows = codes.shape[0] + grads.shape[0]
    whole = lambda shape: pl.BlockSpec(shape, lambda *_: (0,) * len(shape))
    return pl.pallas_call(
        pack_kernel,
        out_shape=jax.ShapeDtypeStruct((slots, rows, span), jnp.bfloat16),
        grid_spec=pltpu.PrefetchScalarGridSpec(
            num_scalar_prefetch=2,
            grid=(1,),
            in_specs=[whole(ids.shape), whole(codes.shape), whole(grads.shape)],
            out_specs=whole((slots, rows, span)),
        ),
        compiler_params=pltpu.CompilerParams(vmem_limit_bytes=48 << 20),
        name="pack_windows",
    )(starts, nodes, ids, codes, grads)


def hist_kernel(order, total, recv_ref, out_ref, codes_ref, grads_ref):
    features = out_ref.shape[1] // BINS
    outputs = out_ref.shape[0]
    per_panel = recv_ref.shape[2] // LANES
    most = grads_ref.shape[0] // (2 * LANES)

    def gather(i, _):
        block = order[i]
        panel = block // per_panel
        at = pl.multiple_of((block % per_panel) * LANES, LANES)
        to = pl.multiple_of(i * LANES, LANES)
        codes_ref[:, pl.ds(to, LANES)] = recv_ref[panel, :features, pl.ds(at, LANES)].astype(jnp.float32)
        tile = recv_ref[panel, features:, pl.ds(at, LANES)].astype(jnp.float32)
        grads_ref[pl.ds(to, LANES), :] = tile.T.astype(jnp.bfloat16)
        return 0

    count = total[0]
    lax.fori_loop(0, count, gather, 0)
    steps = (count + 1) // 2

    @pl.when(count % 2 == 1)
    def _():
        to = pl.multiple_of(count * LANES, LANES)
        codes_ref[:, pl.ds(to, LANES)] = jnp.full((features, LANES), OUTSIDE, jnp.float32)
        grads_ref[pl.ds(to, LANES), :] = jnp.zeros((LANES, outputs), jnp.bfloat16)

    @pl.when(count == 0)
    def _():
        out_ref[...] = jnp.zeros_like(out_ref)

    def body(depth, first, add):
        base = lax.broadcasted_iota(jnp.int32, (16, depth), 0).astype(jnp.float32)

        def one(g, _):
            parts = []
            for q in range(GROUP):
                row = codes_ref[pl.ds(g * GROUP + q, 1), pl.ds(first, depth)]
                rows = (jnp.broadcast_to(row, (16, depth)) - base).astype(jnp.bfloat16)
                for b in range(BINS // 16):
                    parts.append(jnp.where(rows == jnp.bfloat16(16 * b), jnp.bfloat16(1), jnp.bfloat16(0)))
            table = jnp.concatenate(parts, axis=0)
            tile = jnp.dot(table, grads_ref[pl.ds(first, depth), :], preferred_element_type=jnp.float32).T
            at = pl.ds(pl.multiple_of(g * GROUP * BINS, GROUP * BINS), GROUP * BINS)
            out_ref[:, at] = out_ref[:, at] + tile if add else tile
            return 0

        lax.fori_loop(0, features // GROUP, one, 0)

    if most <= CHUNK:
        for n in range(1, most + 1):
            pl.when(steps == n)(functools.partial(body, n * 2 * LANES, 0, False))
        return

    out_ref[...] = jnp.zeros_like(out_ref)

    def chunk(c, _):
        first = pl.multiple_of(c * CHUNK * 2 * LANES, LANES)
        here = jnp.minimum(steps - c * CHUNK, CHUNK)
        for n in range(1, CHUNK + 1):
            pl.when(here == n)(functools.partial(body, n * 2 * LANES, first, True))
        return 0

    lax.fori_loop(0, (steps + CHUNK - 1) // CHUNK, chunk, 0)


def node_histogram(order, total, recv, features, outputs):
    panels, rows, span = recv.shape
    blocks = panels * (span // LANES)
    depth = (blocks + 1) // 2 * 2 * LANES
    return pl.pallas_call(
        hist_kernel,
        out_shape=jax.ShapeDtypeStruct((outputs, features * BINS), jnp.float32),
        grid_spec=pltpu.PrefetchScalarGridSpec(
            num_scalar_prefetch=2,
            grid=(1,),
            in_specs=[pl.BlockSpec((panels, rows, span), lambda *_: (0, 0, 0))],
            out_specs=pl.BlockSpec((outputs, features * BINS), lambda *_: (0, 0)),
            scratch_shapes=[
                pltpu.VMEM((features, depth), jnp.float32),
                pltpu.VMEM((depth, outputs), jnp.bfloat16),
            ],
        ),
        compiler_params=pltpu.CompilerParams(vmem_limit_bytes=56 << 20),
        name="node_histogram",
    )(order, total, recv)


def on_device(grads, codes, node_ids, node_slot):
    gathered = lax.all_gather(grads, "feat", axis=1, tiled=True)
    total_nodes = node_slot.shape[0]
    features, length = codes.shape
    outputs = grads.shape[0]
    capacity = 2 * length // total_nodes
    span = capacity + LANES
    row_starts = jnp.sum((node_ids[None, :] < node_slot[:, None]).astype(jnp.int32), axis=1)
    starts = jnp.minimum(row_starts // LANES * LANES, length - span)
    sent = pack_windows(starts, node_slot, node_ids.reshape(1, length), codes, gathered, span)
    recv = lax.all_to_all(sent, "row", split_axis=0, concat_axis=0, tiled=True)
    blocks = recv.shape[0] * (span // LANES)
    filled = (recv[:, 0, :] < BINS).reshape(blocks, LANES).any(axis=1)
    index = jnp.arange(blocks, dtype=jnp.int32)
    rank = jnp.sum((filled[None, :] & (index[None, :] < index[:, None])).astype(jnp.int32), axis=1)
    hit = filled[None, :] & (rank[None, :] == index[:, None])
    order = jnp.sum(jnp.where(hit, index[None, :], 0), axis=1)
    total = jnp.sum(filled.astype(jnp.int32)).reshape(1)
    return node_histogram(order, total, recv, features, outputs)[None]


def solution(mesh):
    in_specs = (P(None, ("row", "feat")), P("feat", "row"), P("row"), P())
    out_specs = P("row", None, "feat")
    return jax.shard_map(
        on_device, mesh=mesh, in_specs=in_specs, out_specs=out_specs, check_vma=False
    )
```

```python
import functools

import jax
import jax.numpy as jnp
from jax import lax
from jax.experimental import pallas as pl
from jax.experimental.pallas import tpu as pltpu
from jax.sharding import PartitionSpec as P

BINS = 128
LANES = 128
OUTSIDE = 255
MESH = pl.DeviceIdType.MESH
GROUP = 4
CHUNK = 16


def around(count, start, body):
    lax.fori_loop(1, count, lambda d, _: (body(lax.rem(start + d, count)), 0)[1], 0)


def regroup_kernel(grads_ref, out_ref, send, recv, own_sem):
    groups, _, piece = grads_ref.shape
    row, feat = lax.axis_index("row"), lax.axis_index("feat")

    def part(owner):
        return out_ref.at[:, pl.ds(pl.multiple_of(owner * piece, LANES), piece)]

    def copy(peer, owner):
        return pltpu.make_async_remote_copy(
            grads_ref.at[peer], part(owner), send.at[peer], recv.at[owner], (row, peer), MESH
        )

    barrier = pltpu.get_barrier_semaphore()
    around(groups, feat, lambda f: pl.semaphore_signal(barrier, 1, device_id=(row, f), device_id_type=MESH))
    own = pltpu.make_async_copy(grads_ref.at[feat], part(feat), own_sem)
    own.start()
    pl.semaphore_wait(barrier, groups - 1)
    around(groups, feat, lambda f: copy(f, feat).start())
    own.wait()
    around(groups, feat, lambda f: copy(feat, f).wait_recv())
    around(groups, feat, lambda f: copy(f, feat).wait_send())


def regroup(grads):
    groups = lax.axis_size("feat")
    outputs, piece = grads.shape
    share = outputs // groups
    vectors = pl.BlockSpec(memory_space=pltpu.VMEM)
    return pl.pallas_call(
        regroup_kernel,
        out_shape=jax.ShapeDtypeStruct((share, groups * piece), jnp.bfloat16),
        in_specs=[vectors],
        out_specs=vectors,
        scratch_shapes=[
            pltpu.SemaphoreType.DMA((groups,)),
            pltpu.SemaphoreType.DMA((groups,)),
            pltpu.SemaphoreType.DMA,
        ],
        compiler_params=pltpu.CompilerParams(collective_id=0, has_side_effects=True),
        name="regroup",
    )(grads.reshape(groups, share, piece))


def pack_kernel(starts, offsets, nodes, ids_ref, codes_ref, grads_ref, codes_out, grads_out):
    slots, _, capacity = codes_out.shape
    span = capacity + LANES
    for j in range(slots):
        window = pl.ds(pl.multiple_of(starts[j], LANES), span)
        inside = ids_ref[:, window] == nodes[j]
        part = codes_ref[:, window]
        part = jnp.where(jnp.broadcast_to(inside, part.shape), part, OUTSIDE)
        codes_out[j] = pltpu.roll(part, offsets[j], 1)[:, :capacity].astype(jnp.float32).astype(jnp.bfloat16)
        part = grads_ref[:, window].astype(jnp.float32)
        grads_out[j] = pltpu.roll(part, offsets[j], 1)[:, :capacity].astype(jnp.bfloat16)


def pack_windows(starts, offsets, nodes, ids, codes, grads, capacity):
    slots = starts.shape[0]
    scalars = pl.BlockSpec(memory_space=pltpu.SMEM)
    vectors = pl.BlockSpec(memory_space=pltpu.VMEM)
    return pl.pallas_call(
        pack_kernel,
        out_shape=(
            jax.ShapeDtypeStruct((slots, codes.shape[0], capacity), jnp.bfloat16),
            jax.ShapeDtypeStruct((slots, grads.shape[0], capacity), jnp.bfloat16),
        ),
        in_specs=[scalars] * 3 + [vectors] * 3,
        out_specs=(vectors, vectors),
        compiler_params=pltpu.CompilerParams(vmem_limit_bytes=40 << 20),
        name="pack_windows",
    )(starts, offsets, nodes, ids, codes, grads)


def exchange_kernel(
    codes_sent, grads_sent, codes_out, grads_out, code_send, code_recv,
    grad_send, grad_recv, spread_send, spread_recv, own_sem,
):
    owners, groups = grads_out.shape[:2]
    row, feat = lax.axis_index("row"), lax.axis_index("feat")

    def code_copy(peer, owner):
        return pltpu.make_async_remote_copy(
            codes_sent.at[peer], codes_out.at[owner],
            code_send.at[peer], code_recv.at[owner], (peer, feat), MESH,
        )

    def grad_copy(peer, owner):
        return pltpu.make_async_remote_copy(
            grads_sent.at[peer], grads_out.at[owner, feat],
            grad_send.at[peer], grad_recv.at[owner], (peer, feat), MESH,
        )

    def spread_copy(panel, peer, owner):
        return pltpu.make_async_remote_copy(
            grads_out.at[panel, owner], grads_out.at[panel, owner],
            spread_send.at[panel, peer], spread_recv.at[panel, owner], (row, peer), MESH,
        )

    def every_panel(body):
        lax.fori_loop(0, owners, lambda p, _: (around(groups, feat, lambda f: body(p, f)), 0)[1], 0)

    barrier = pltpu.get_barrier_semaphore()
    around(groups, feat, lambda f: pl.semaphore_signal(barrier, 1, device_id=(row, f), device_id_type=MESH))
    around(owners, row, lambda r: pl.semaphore_signal(barrier, 1, device_id=(r, feat), device_id_type=MESH))
    own_grads = pltpu.make_async_copy(grads_sent.at[row], grads_out.at[row, feat], own_sem.at[0])
    own_codes = pltpu.make_async_copy(codes_sent.at[row], codes_out.at[row], own_sem.at[1])
    own_grads.start()
    own_codes.start()
    pl.semaphore_wait(barrier, owners + groups - 2)
    around(owners, row, lambda r: grad_copy(r, row).start())
    around(owners, row, lambda r: code_copy(r, row).start())
    own_grads.wait()
    around(groups, feat, lambda f: spread_copy(row, f, feat).start())

    def spread(panel):
        grad_copy(row, panel).wait_recv()
        around(groups, feat, lambda f: spread_copy(panel, f, feat).start())

    around(owners, row, spread)
    own_codes.wait()
    around(owners, row, lambda r: code_copy(row, r).wait_recv())
    every_panel(lambda p, f: spread_copy(p, feat, f).wait_recv())
    around(owners, row, lambda r: code_copy(r, row).wait_send())
    around(owners, row, lambda r: grad_copy(r, row).wait_send())
    every_panel(lambda p, f: spread_copy(p, f, feat).wait_send())


def exchange(codes, grads):
    groups = lax.axis_size("feat")
    owners, _, capacity = codes.shape
    vectors = pl.BlockSpec(memory_space=pltpu.VMEM)
    return pl.pallas_call(
        exchange_kernel,
        out_shape=(
            jax.ShapeDtypeStruct(codes.shape, jnp.bfloat16),
            jax.ShapeDtypeStruct((owners, groups, grads.shape[1], capacity), jnp.bfloat16),
        ),
        in_specs=[vectors] * 2,
        out_specs=(vectors, vectors),
        scratch_shapes=[pltpu.SemaphoreType.DMA((owners,))] * 4
        + [pltpu.SemaphoreType.DMA((owners, groups))] * 2
        + [pltpu.SemaphoreType.DMA((2,))],
        compiler_params=pltpu.CompilerParams(
            collective_id=1, has_side_effects=True, vmem_limit_bytes=40 << 20
        ),
        name="exchange",
    )(codes, grads)


def hist_kernel(order, total, codes_in, grads_in, out_ref, codes_ref, grads_ref):
    features = out_ref.shape[1] // BINS
    outputs = out_ref.shape[0]
    per_panel = codes_in.shape[2] // LANES
    most = grads_ref.shape[0] // (2 * LANES)

    def gather(i, _):
        block = order[i]
        panel = block // per_panel
        at = pl.multiple_of((block % per_panel) * LANES, LANES)
        to = pl.multiple_of(i * LANES, LANES)
        codes_ref[:, pl.ds(to, LANES)] = codes_in[panel, :, pl.ds(at, LANES)].astype(jnp.float32)
        tile = grads_in[panel, :, pl.ds(at, LANES)].astype(jnp.float32)
        grads_ref[pl.ds(to, LANES), :] = tile.T.astype(jnp.bfloat16)
        return 0

    count = total[0]
    lax.fori_loop(0, count, gather, 0)
    steps = (count + 1) // 2

    @pl.when(count % 2 == 1)
    def _():
        to = pl.multiple_of(count * LANES, LANES)
        codes_ref[:, pl.ds(to, LANES)] = jnp.full((features, LANES), OUTSIDE, jnp.float32)
        grads_ref[pl.ds(to, LANES), :] = jnp.zeros((LANES, outputs), jnp.bfloat16)

    @pl.when(count == 0)
    def _():
        out_ref[...] = jnp.zeros_like(out_ref)

    def body(depth, first, add):
        base = lax.broadcasted_iota(jnp.int32, (16, depth), 0).astype(jnp.float32)

        def one(g, _):
            parts = []
            for q in range(GROUP):
                row = codes_ref[pl.ds(g * GROUP + q, 1), pl.ds(first, depth)]
                rows = (jnp.broadcast_to(row, (16, depth)) - base).astype(jnp.bfloat16)
                for b in range(BINS // 16):
                    parts.append(jnp.where(rows == jnp.bfloat16(16 * b), jnp.bfloat16(1), jnp.bfloat16(0)))
            table = jnp.concatenate(parts, axis=0)
            tile = jnp.dot(table, grads_ref[pl.ds(first, depth), :], preferred_element_type=jnp.float32).T
            at = pl.ds(pl.multiple_of(g * GROUP * BINS, GROUP * BINS), GROUP * BINS)
            out_ref[:, at] = out_ref[:, at] + tile if add else tile
            return 0

        lax.fori_loop(0, features // GROUP, one, 0)

    if most <= CHUNK:
        for n in range(1, most + 1):
            pl.when(steps == n)(functools.partial(body, n * 2 * LANES, 0, False))
        return

    out_ref[...] = jnp.zeros_like(out_ref)

    def chunk(c, _):
        first = pl.multiple_of(c * CHUNK * 2 * LANES, LANES)
        here = jnp.minimum(steps - c * CHUNK, CHUNK)
        for n in range(1, CHUNK + 1):
            pl.when(here == n)(functools.partial(body, n * 2 * LANES, first, True))
        return 0

    lax.fori_loop(0, (steps + CHUNK - 1) // CHUNK, chunk, 0)


def node_histogram(order, total, codes, grads):
    panels, features, capacity = codes.shape
    outputs = grads.shape[1]
    blocks = panels * (capacity // LANES)
    depth = (blocks + 1) // 2 * 2 * LANES
    return pl.pallas_call(
        hist_kernel,
        out_shape=jax.ShapeDtypeStruct((outputs, features * BINS), jnp.float32),
        grid_spec=pltpu.PrefetchScalarGridSpec(
            num_scalar_prefetch=2,
            grid=(1,),
            in_specs=[
                pl.BlockSpec(codes.shape, lambda *_: (0, 0, 0)),
                pl.BlockSpec(grads.shape, lambda *_: (0, 0, 0)),
            ],
            out_specs=pl.BlockSpec((outputs, features * BINS), lambda *_: (0, 0)),
            scratch_shapes=[
                pltpu.VMEM((features, depth), jnp.float32),
                pltpu.VMEM((depth, outputs), jnp.bfloat16),
            ],
        ),
        compiler_params=pltpu.CompilerParams(vmem_limit_bytes=56 << 20),
        name="node_histogram",
    )(order, total, codes, grads)


def on_device(grads, codes, node_ids, node_slot):
    total_nodes = node_slot.shape[0]
    length = codes.shape[1]
    capacity = 2 * length // total_nodes
    span = capacity + LANES
    row_starts = jnp.sum((node_ids[None, :] < node_slot[:, None]).astype(jnp.int32), axis=1)
    starts = jnp.minimum(row_starts // LANES * LANES, length - span)
    offsets = (span - (row_starts - starts)) % span
    panel = regroup(grads)
    sent = pack_windows(
        starts, offsets, node_slot, node_ids.reshape(1, length), codes, panel, capacity
    )
    codes_in, grads_in = exchange(*sent)
    grads_in = grads_in.reshape(grads_in.shape[0], -1, capacity)
    blocks = codes_in.shape[0] * (capacity // LANES)
    filled = (codes_in[:, 0, :] < BINS).reshape(blocks, LANES).any(axis=1)
    index = jnp.arange(blocks, dtype=jnp.int32)
    rank = jnp.sum((filled[None, :] & (index[None, :] < index[:, None])).astype(jnp.int32), axis=1)
    hit = filled[None, :] & (rank[None, :] == index[:, None])
    order = jnp.sum(jnp.where(hit, index[None, :], 0), axis=1)
    total = jnp.sum(filled.astype(jnp.int32)).reshape(1)
    return node_histogram(order, total, codes_in, grads_in)[None]


def solution(mesh):
    in_specs = (P(None, ("row", "feat")), P("feat", "row"), P("row"), P())
    out_specs = P("row", None, "feat")
    return jax.shard_map(
        on_device, mesh=mesh, in_specs=in_specs, out_specs=out_specs, check_vma=False
    )
```

```python
import functools

import jax
import jax.numpy as jnp
from jax import lax
from jax.experimental import pallas as pl
from jax.experimental.pallas import tpu as pltpu
from jax.sharding import PartitionSpec as P

BINS = 128
LANES = 128
OUTSIDE = 255
MESH = pl.DeviceIdType.MESH
GROUP = 4
CHUNK = 16


def around(count, start, body):
    lax.fori_loop(1, count, lambda d, _: (body(lax.rem(start + d, count)), 0)[1], 0)


def regroup_kernel(grads_ref, codes_ref, out_ref, codes_out, send, recv, own_sem, codes_sem):
    groups, _, piece = grads_ref.shape
    row, feat = lax.axis_index("row"), lax.axis_index("feat")

    def part(owner):
        return out_ref.at[:, pl.ds(pl.multiple_of(owner * piece, LANES), piece)]

    def copy(peer, owner):
        return pltpu.make_async_remote_copy(
            grads_ref.at[peer], part(owner), send.at[peer], recv.at[owner], (row, peer), MESH
        )

    barrier = pltpu.get_barrier_semaphore()
    around(groups, feat, lambda f: pl.semaphore_signal(barrier, 1, device_id=(row, f), device_id_type=MESH))
    own = pltpu.make_async_copy(grads_ref.at[feat], part(feat), own_sem)
    own.start()
    codes = pltpu.make_async_copy(codes_ref, codes_out, codes_sem)
    codes.start()
    pl.semaphore_wait(barrier, groups - 1)
    around(groups, feat, lambda f: copy(f, feat).start())
    own.wait()
    around(groups, feat, lambda f: copy(feat, f).wait_recv())
    around(groups, feat, lambda f: copy(f, feat).wait_send())
    codes.wait()


def regroup(grads, codes):
    groups = lax.axis_size("feat")
    outputs, piece = grads.shape
    share = outputs // groups
    vectors = pl.BlockSpec(memory_space=pltpu.VMEM)
    return pl.pallas_call(
        regroup_kernel,
        out_shape=(
            jax.ShapeDtypeStruct((share, groups * piece), jnp.bfloat16),
            jax.ShapeDtypeStruct(codes.shape, codes.dtype),
        ),
        in_specs=[vectors, pl.BlockSpec(memory_space=pl.ANY)],
        out_specs=(vectors, vectors),
        scratch_shapes=[
            pltpu.SemaphoreType.DMA((groups,)),
            pltpu.SemaphoreType.DMA((groups,)),
            pltpu.SemaphoreType.DMA,
            pltpu.SemaphoreType.DMA,
        ],
        compiler_params=pltpu.CompilerParams(collective_id=0, has_side_effects=True),
        name="regroup",
    )(grads.reshape(groups, share, piece), codes)


def pack_kernel(scalars, ids_ref, codes_ref, grads_ref, codes_out, grads_out):
    slots, _, capacity = codes_out.shape
    span = capacity + LANES
    for j in range(slots):
        window = pl.ds(pl.multiple_of(scalars[0, j], LANES), span)
        inside = ids_ref[:, window] == scalars[2, j]
        part = codes_ref[:, window]
        part = jnp.where(jnp.broadcast_to(inside, part.shape), part, OUTSIDE)
        codes_out[j] = pltpu.roll(part, scalars[1, j], 1)[:, :capacity].astype(jnp.float32).astype(jnp.bfloat16)
        part = grads_ref[:, window].astype(jnp.float32)
        grads_out[j] = pltpu.roll(part, scalars[1, j], 1)[:, :capacity].astype(jnp.bfloat16)


def pack_windows(scalars, ids, codes, grads, capacity):
    slots = scalars.shape[1]
    vectors = pl.BlockSpec(memory_space=pltpu.VMEM)
    return pl.pallas_call(
        pack_kernel,
        out_shape=(
            jax.ShapeDtypeStruct((slots, codes.shape[0], capacity), jnp.bfloat16),
            jax.ShapeDtypeStruct((slots, grads.shape[0], capacity), jnp.bfloat16),
        ),
        in_specs=[pl.BlockSpec(memory_space=pltpu.SMEM)] + [vectors] * 3,
        out_specs=(vectors, vectors),
        compiler_params=pltpu.CompilerParams(vmem_limit_bytes=40 << 20),
        name="pack_windows",
    )(scalars, ids, codes, grads)


def exchange_kernel(
    codes_sent, grads_sent, codes_out, grads_out, code_send, code_recv,
    grad_send, grad_recv, spread_send, spread_recv, own_sem,
):
    owners, groups = grads_out.shape[:2]
    row, feat = lax.axis_index("row"), lax.axis_index("feat")

    def code_copy(peer, owner):
        return pltpu.make_async_remote_copy(
            codes_sent.at[peer], codes_out.at[owner],
            code_send.at[peer], code_recv.at[owner], (peer, feat), MESH,
        )

    def grad_copy(peer, owner):
        return pltpu.make_async_remote_copy(
            grads_sent.at[peer], grads_out.at[owner, feat],
            grad_send.at[peer], grad_recv.at[owner], (peer, feat), MESH,
        )

    def spread_copy(panel, peer, owner):
        return pltpu.make_async_remote_copy(
            grads_out.at[panel, owner], grads_out.at[panel, owner],
            spread_send.at[panel, peer], spread_recv.at[panel, owner], (row, peer), MESH,
        )

    def every_panel(body):
        lax.fori_loop(0, owners, lambda p, _: (around(groups, feat, lambda f: body(p, f)), 0)[1], 0)

    barrier = pltpu.get_barrier_semaphore()
    around(groups, feat, lambda f: pl.semaphore_signal(barrier, 1, device_id=(row, f), device_id_type=MESH))
    around(owners, row, lambda r: pl.semaphore_signal(barrier, 1, device_id=(r, feat), device_id_type=MESH))
    own_grads = pltpu.make_async_copy(grads_sent.at[row], grads_out.at[row, feat], own_sem.at[0])
    own_codes = pltpu.make_async_copy(codes_sent.at[row], codes_out.at[row], own_sem.at[1])
    own_grads.start()
    own_codes.start()
    pl.semaphore_wait(barrier, owners + groups - 2)
    around(owners, row, lambda r: grad_copy(r, row).start())
    around(owners, row, lambda r: code_copy(r, row).start())
    own_grads.wait()
    around(groups, feat, lambda f: spread_copy(row, f, feat).start())

    def spread(panel):
        grad_copy(row, panel).wait_recv()
        around(groups, feat, lambda f: spread_copy(panel, f, feat).start())

    around(owners, row, spread)
    own_codes.wait()
    around(owners, row, lambda r: code_copy(row, r).wait_recv())
    every_panel(lambda p, f: spread_copy(p, feat, f).wait_recv())
    around(owners, row, lambda r: code_copy(r, row).wait_send())
    around(owners, row, lambda r: grad_copy(r, row).wait_send())
    every_panel(lambda p, f: spread_copy(p, f, feat).wait_send())


def exchange(codes, grads):
    groups = lax.axis_size("feat")
    owners, _, capacity = codes.shape
    vectors = pl.BlockSpec(memory_space=pltpu.VMEM)
    return pl.pallas_call(
        exchange_kernel,
        out_shape=(
            jax.ShapeDtypeStruct(codes.shape, jnp.bfloat16),
            jax.ShapeDtypeStruct((owners, groups, grads.shape[1], capacity), jnp.bfloat16),
        ),
        in_specs=[vectors] * 2,
        out_specs=(vectors, vectors),
        scratch_shapes=[pltpu.SemaphoreType.DMA((owners,))] * 4
        + [pltpu.SemaphoreType.DMA((owners, groups))] * 2
        + [pltpu.SemaphoreType.DMA((2,))],
        compiler_params=pltpu.CompilerParams(
            collective_id=1, has_side_effects=True, vmem_limit_bytes=40 << 20
        ),
        name="exchange",
    )(codes, grads)


def hist_kernel(counts, codes_in, grads_in, out_ref, codes_ref, lines_ref, grads_ref):
    panels, features, capacity = codes_in.shape
    outputs = out_ref.shape[0]
    span = capacity + LANES
    step = 2 * LANES
    most = (panels * capacity + step - 1) // step

    def append(p, filled):
        shift = filled % LANES
        at = pl.ds(pl.multiple_of(filled // LANES * LANES, LANES), span)

        def place(ref, part, fill):
            rest = jnp.full((part.shape[0], LANES), fill, jnp.float32)
            moved = pltpu.roll(jnp.concatenate([part.astype(jnp.float32), rest], axis=1), shift, 1)
            lane = lax.broadcasted_iota(jnp.int32, moved.shape, 1)
            ref[:, at] = jnp.where(lane < shift, ref[:, at], moved)

        place(codes_ref, codes_in[p], float(OUTSIDE))
        place(lines_ref, grads_in[p], 0.0)
        return filled + counts[p]

    filled = lax.fori_loop(0, panels, append, 0)
    steps = (filled + step - 1) // step
    tail = pl.ds(pl.multiple_of((filled + LANES - 1) // LANES * LANES, LANES), LANES)
    codes_ref[:, tail] = jnp.full((features, LANES), OUTSIDE, jnp.float32)
    lines_ref[:, tail] = jnp.zeros((outputs, LANES), jnp.float32)

    def turn(i, _):
        at = pl.ds(pl.multiple_of(i * step, step), step)
        grads_ref[at, :] = lines_ref[:, at].T.astype(jnp.bfloat16)
        return 0

    lax.fori_loop(0, steps, turn, 0)

    @pl.when(filled == 0)
    def _():
        out_ref[...] = jnp.zeros_like(out_ref)

    def body(depth, first, add):
        base = lax.broadcasted_iota(jnp.int32, (16, depth), 0).astype(jnp.float32)

        def one(g, _):
            parts = []
            for q in range(GROUP):
                row = codes_ref[pl.ds(g * GROUP + q, 1), pl.ds(first, depth)]
                rows = (jnp.broadcast_to(row, (16, depth)) - base).astype(jnp.bfloat16)
                for b in range(BINS // 16):
                    parts.append(jnp.where(rows == jnp.bfloat16(16 * b), jnp.bfloat16(1), jnp.bfloat16(0)))
            table = jnp.concatenate(parts, axis=0)
            tile = jnp.dot(table, grads_ref[pl.ds(first, depth), :], preferred_element_type=jnp.float32).T
            at = pl.ds(pl.multiple_of(g * GROUP * BINS, GROUP * BINS), GROUP * BINS)
            out_ref[:, at] = out_ref[:, at] + tile if add else tile
            return 0

        lax.fori_loop(0, features // GROUP, one, 0)

    if most <= CHUNK:
        for n in range(1, most + 1):
            pl.when(steps == n)(functools.partial(body, n * 2 * LANES, 0, False))
        return

    out_ref[...] = jnp.zeros_like(out_ref)

    def chunk(c, _):
        first = pl.multiple_of(c * CHUNK * 2 * LANES, LANES)
        here = jnp.minimum(steps - c * CHUNK, CHUNK)
        for n in range(1, CHUNK + 1):
            pl.when(here == n)(functools.partial(body, n * 2 * LANES, first, True))
        return 0

    lax.fori_loop(0, (steps + CHUNK - 1) // CHUNK, chunk, 0)


def node_histogram(counts, codes, grads):
    panels, features, capacity = codes.shape
    outputs = grads.shape[1]
    depth = panels * capacity + capacity + 2 * LANES
    vectors = pl.BlockSpec(memory_space=pltpu.VMEM)
    return pl.pallas_call(
        hist_kernel,
        out_shape=jax.ShapeDtypeStruct((outputs, features * BINS), jnp.float32),
        in_specs=[pl.BlockSpec(memory_space=pltpu.SMEM), vectors, vectors],
        out_specs=vectors,
        scratch_shapes=[
            pltpu.VMEM((features, depth), jnp.float32),
            pltpu.VMEM((outputs, depth), jnp.float32),
            pltpu.VMEM((depth, outputs), jnp.bfloat16),
        ],
        compiler_params=pltpu.CompilerParams(vmem_limit_bytes=56 << 20),
        name="node_histogram",
    )(counts, codes, grads)


def on_device(grads, codes, node_ids, node_slot):
    total_nodes = node_slot.shape[0]
    length = codes.shape[1]
    capacity = 2 * length // total_nodes
    span = capacity + LANES
    row_starts = jnp.sum((node_ids[None, :] < node_slot[:, None]).astype(jnp.int32), axis=1)
    starts = jnp.minimum(row_starts // LANES * LANES, length - span)
    offsets = (span - (row_starts - starts)) % span
    scalars = jnp.stack([starts, offsets, node_slot])
    panel, codes = regroup(grads, codes)
    sent = pack_windows(scalars, node_ids.reshape(1, length), codes, panel, capacity)
    codes_in, grads_in = exchange(*sent)
    grads_in = grads_in.reshape(grads_in.shape[0], -1, capacity)
    counts = jnp.sum((codes_in[:, 0, :] < BINS).astype(jnp.int32), axis=1)
    return node_histogram(counts, codes_in, grads_in)[None]


def solution(mesh):
    in_specs = (P(None, ("row", "feat")), P("feat", "row"), P("row"), P())
    out_specs = P("row", None, "feat")
    return jax.shard_map(
        on_device, mesh=mesh, in_specs=in_specs, out_specs=out_specs, check_vma=False
    )
```

```python
import functools

import jax
import jax.numpy as jnp
from jax import lax
from jax.experimental import pallas as pl
from jax.experimental.pallas import tpu as pltpu
from jax.sharding import PartitionSpec as P

BINS = 128
LANES = 128
OUTSIDE = 255
MESH = pl.DeviceIdType.MESH
GROUP = 4
CHUNK = 16


def around(count, start, body):
    lax.fori_loop(1, count, lambda d, _: (body(lax.rem(start + d, count)), 0)[1], 0)


def regroup_kernel(grads_ref, codes_ref, out_ref, codes_out, send, recv, own_sem, codes_sem):
    groups, _, piece = grads_ref.shape
    row, feat = lax.axis_index("row"), lax.axis_index("feat")

    def part(owner):
        return out_ref.at[:, pl.ds(pl.multiple_of(owner * piece, LANES), piece)]

    def copy(peer, owner):
        return pltpu.make_async_remote_copy(
            grads_ref.at[peer], part(owner), send.at[peer], recv.at[owner], (row, peer), MESH
        )

    barrier = pltpu.get_barrier_semaphore()
    around(groups, feat, lambda f: pl.semaphore_signal(barrier, 1, device_id=(row, f), device_id_type=MESH))
    own = pltpu.make_async_copy(grads_ref.at[feat], part(feat), own_sem)
    own.start()
    codes = pltpu.make_async_copy(codes_ref, codes_out, codes_sem)
    codes.start()
    pl.semaphore_wait(barrier, groups - 1)
    around(groups, feat, lambda f: copy(f, feat).start())
    own.wait()
    around(groups, feat, lambda f: copy(feat, f).wait_recv())
    around(groups, feat, lambda f: copy(f, feat).wait_send())
    codes.wait()


def regroup(grads, codes):
    groups = lax.axis_size("feat")
    outputs, piece = grads.shape
    share = outputs // groups
    vectors = pl.BlockSpec(memory_space=pltpu.VMEM)
    return pl.pallas_call(
        regroup_kernel,
        out_shape=(
            jax.ShapeDtypeStruct((share, groups * piece), jnp.bfloat16),
            jax.ShapeDtypeStruct(codes.shape, codes.dtype),
        ),
        in_specs=[vectors, pl.BlockSpec(memory_space=pl.ANY)],
        out_specs=(vectors, vectors),
        scratch_shapes=[
            pltpu.SemaphoreType.DMA((groups,)),
            pltpu.SemaphoreType.DMA((groups,)),
            pltpu.SemaphoreType.DMA,
            pltpu.SemaphoreType.DMA,
        ],
        compiler_params=pltpu.CompilerParams(
            collective_id=0, has_side_effects=True, vmem_limit_bytes=8 << 20
        ),
        name="regroup",
    )(grads.reshape(groups, share, piece), codes)


def pack_kernel(scalars, ids_ref, codes_ref, grads_ref, codes_out, grads_out):
    slots, _, capacity = codes_out.shape
    span = capacity + LANES
    for j in range(slots):
        window = pl.ds(pl.multiple_of(scalars[0, j], LANES), span)
        inside = ids_ref[:, window] == scalars[2, j]
        part = codes_ref[:, window]
        part = jnp.where(jnp.broadcast_to(inside, part.shape), part, OUTSIDE)
        codes_out[j] = pltpu.roll(part, scalars[1, j], 1)[:, :capacity].astype(jnp.float32).astype(jnp.bfloat16)
        part = grads_ref[:, window].astype(jnp.float32)
        grads_out[j] = pltpu.roll(part, scalars[1, j], 1)[:, :capacity].astype(jnp.bfloat16)


def pack_windows(scalars, ids, codes, grads, capacity):
    slots = scalars.shape[1]
    vectors = pl.BlockSpec(memory_space=pltpu.VMEM)
    return pl.pallas_call(
        pack_kernel,
        out_shape=(
            jax.ShapeDtypeStruct((slots, codes.shape[0], capacity), jnp.bfloat16),
            jax.ShapeDtypeStruct((slots, grads.shape[0], capacity), jnp.bfloat16),
        ),
        in_specs=[pl.BlockSpec(memory_space=pltpu.SMEM)] + [vectors] * 3,
        out_specs=(vectors, vectors),
        compiler_params=pltpu.CompilerParams(vmem_limit_bytes=12 << 20),
        name="pack_windows",
    )(scalars, ids, codes, grads)


def exchange_kernel(
    codes_sent, grads_sent, codes_out, grads_out, code_send, code_recv,
    grad_send, grad_recv, spread_send, spread_recv, own_sem,
):
    owners, groups = grads_out.shape[:2]
    row, feat = lax.axis_index("row"), lax.axis_index("feat")

    def code_copy(peer, owner):
        return pltpu.make_async_remote_copy(
            codes_sent.at[peer], codes_out.at[owner],
            code_send.at[peer], code_recv.at[owner], (peer, feat), MESH,
        )

    def grad_copy(peer, owner):
        return pltpu.make_async_remote_copy(
            grads_sent.at[peer], grads_out.at[owner, feat],
            grad_send.at[peer], grad_recv.at[owner], (peer, feat), MESH,
        )

    def spread_copy(panel, peer, owner):
        return pltpu.make_async_remote_copy(
            grads_out.at[panel, owner], grads_out.at[panel, owner],
            spread_send.at[panel, peer], spread_recv.at[panel, owner], (row, peer), MESH,
        )

    def every_panel(body):
        lax.fori_loop(0, owners, lambda p, _: (around(groups, feat, lambda f: body(p, f)), 0)[1], 0)

    barrier = pltpu.get_barrier_semaphore()
    around(groups, feat, lambda f: pl.semaphore_signal(barrier, 1, device_id=(row, f), device_id_type=MESH))
    around(owners, row, lambda r: pl.semaphore_signal(barrier, 1, device_id=(r, feat), device_id_type=MESH))
    own_grads = pltpu.make_async_copy(grads_sent.at[row], grads_out.at[row, feat], own_sem.at[0])
    own_codes = pltpu.make_async_copy(codes_sent.at[row], codes_out.at[row], own_sem.at[1])
    own_grads.start()
    own_codes.start()
    pl.semaphore_wait(barrier, owners + groups - 2)
    around(owners, row, lambda r: grad_copy(r, row).start())
    around(owners, row, lambda r: code_copy(r, row).start())
    own_grads.wait()
    around(groups, feat, lambda f: spread_copy(row, f, feat).start())

    def spread(panel):
        grad_copy(row, panel).wait_recv()
        around(groups, feat, lambda f: spread_copy(panel, f, feat).start())

    around(owners, row, spread)
    own_codes.wait()
    around(owners, row, lambda r: code_copy(row, r).wait_recv())
    every_panel(lambda p, f: spread_copy(p, feat, f).wait_recv())
    around(owners, row, lambda r: code_copy(r, row).wait_send())
    around(owners, row, lambda r: grad_copy(r, row).wait_send())
    every_panel(lambda p, f: spread_copy(p, f, feat).wait_send())


def exchange(codes, grads):
    groups = lax.axis_size("feat")
    owners, _, capacity = codes.shape
    vectors = pl.BlockSpec(memory_space=pltpu.VMEM)
    return pl.pallas_call(
        exchange_kernel,
        out_shape=(
            jax.ShapeDtypeStruct(codes.shape, jnp.bfloat16),
            jax.ShapeDtypeStruct((owners, groups, grads.shape[1], capacity), jnp.bfloat16),
        ),
        in_specs=[vectors] * 2,
        out_specs=(vectors, vectors),
        scratch_shapes=[pltpu.SemaphoreType.DMA((owners,))] * 4
        + [pltpu.SemaphoreType.DMA((owners, groups))] * 2
        + [pltpu.SemaphoreType.DMA((2,))],
        compiler_params=pltpu.CompilerParams(
            collective_id=1, has_side_effects=True, vmem_limit_bytes=12 << 20
        ),
        name="exchange",
    )(codes, grads)


def hist_kernel(counts, codes_in, grads_in, out_ref, codes_ref, lines_ref, grads_ref):
    panels, features, capacity = codes_in.shape
    outputs = out_ref.shape[0]
    span = capacity + LANES
    step = 2 * LANES
    most = (panels * capacity + step - 1) // step

    def append(p, filled):
        shift = filled % LANES
        at = pl.ds(pl.multiple_of(filled // LANES * LANES, LANES), span)

        def place(ref, part, fill):
            rest = jnp.full((part.shape[0], LANES), fill, jnp.float32)
            moved = pltpu.roll(jnp.concatenate([part.astype(jnp.float32), rest], axis=1), shift, 1)
            lane = lax.broadcasted_iota(jnp.int32, moved.shape, 1)
            ref[:, at] = jnp.where(lane < shift, ref[:, at], moved)

        place(codes_ref, codes_in[p], float(OUTSIDE))
        place(lines_ref, grads_in[p], 0.0)
        return filled + counts[p]

    filled = lax.fori_loop(0, panels, append, 0)
    steps = (filled + step - 1) // step
    tail = pl.ds(pl.multiple_of((filled + LANES - 1) // LANES * LANES, LANES), LANES)
    codes_ref[:, tail] = jnp.full((features, LANES), OUTSIDE, jnp.float32)
    lines_ref[:, tail] = jnp.zeros((outputs, LANES), jnp.float32)

    def turn(i, _):
        at = pl.ds(pl.multiple_of(i * step, step), step)
        grads_ref[at, :] = lines_ref[:, at].T.astype(jnp.bfloat16)
        return 0

    lax.fori_loop(0, steps, turn, 0)

    @pl.when(filled == 0)
    def _():
        out_ref[...] = jnp.zeros_like(out_ref)

    def body(depth, first, add):
        base = lax.broadcasted_iota(jnp.int32, (16, depth), 0).astype(jnp.float32)

        def one(g, _):
            parts = []
            for q in range(GROUP):
                row = codes_ref[pl.ds(g * GROUP + q, 1), pl.ds(first, depth)]
                rows = (jnp.broadcast_to(row, (16, depth)) - base).astype(jnp.bfloat16)
                for b in range(BINS // 16):
                    parts.append(jnp.where(rows == jnp.bfloat16(16 * b), jnp.bfloat16(1), jnp.bfloat16(0)))
            table = jnp.concatenate(parts, axis=0)
            tile = jnp.dot(table, grads_ref[pl.ds(first, depth), :], preferred_element_type=jnp.float32).T
            at = pl.ds(pl.multiple_of(g * GROUP * BINS, GROUP * BINS), GROUP * BINS)
            out_ref[:, at] = out_ref[:, at] + tile if add else tile
            return 0

        lax.fori_loop(0, features // GROUP, one, 0)

    if most <= CHUNK:
        for n in range(1, most + 1):
            pl.when(steps == n)(functools.partial(body, n * 2 * LANES, 0, False))
        return

    out_ref[...] = jnp.zeros_like(out_ref)

    def chunk(c, _):
        first = pl.multiple_of(c * CHUNK * 2 * LANES, LANES)
        here = jnp.minimum(steps - c * CHUNK, CHUNK)
        for n in range(1, CHUNK + 1):
            pl.when(here == n)(functools.partial(body, n * 2 * LANES, first, True))
        return 0

    lax.fori_loop(0, (steps + CHUNK - 1) // CHUNK, chunk, 0)


def node_histogram(counts, codes, grads):
    panels, features, capacity = codes.shape
    outputs = grads.shape[1]
    depth = panels * capacity + capacity + 2 * LANES
    vectors = pl.BlockSpec(memory_space=pltpu.VMEM)
    return pl.pallas_call(
        hist_kernel,
        out_shape=jax.ShapeDtypeStruct((outputs, features * BINS), jnp.float32),
        in_specs=[pl.BlockSpec(memory_space=pltpu.SMEM), vectors, vectors],
        out_specs=vectors,
        scratch_shapes=[
            pltpu.VMEM((features, depth), jnp.float32),
            pltpu.VMEM((outputs, depth), jnp.float32),
            pltpu.VMEM((depth, outputs), jnp.bfloat16),
        ],
        compiler_params=pltpu.CompilerParams(vmem_limit_bytes=24 << 20),
        name="node_histogram",
    )(counts, codes, grads)


def on_device(grads, codes, node_ids, node_slot):
    total_nodes = node_slot.shape[0]
    length = codes.shape[1]
    capacity = 2 * length // total_nodes
    span = capacity + LANES
    row_starts = jnp.sum((node_ids[None, :] < node_slot[:, None]).astype(jnp.int32), axis=1)
    starts = jnp.minimum(row_starts // LANES * LANES, length - span)
    offsets = (span - (row_starts - starts)) % span
    scalars = jnp.stack([starts, offsets, node_slot])
    panel, codes = regroup(grads, codes)
    sent = pack_windows(scalars, node_ids.reshape(1, length), codes, panel, capacity)
    codes_in, grads_in = exchange(*sent)
    grads_in = grads_in.reshape(grads_in.shape[0], -1, capacity)
    counts = jnp.sum((codes_in[:, 0, :] < BINS).astype(jnp.int32), axis=1)
    return node_histogram(counts, codes_in, grads_in)[None]


def solution(mesh):
    in_specs = (P(None, ("row", "feat")), P("feat", "row"), P("row"), P())
    out_specs = P("row", None, "feat")
    return jax.shard_map(
        on_device, mesh=mesh, in_specs=in_specs, out_specs=out_specs, check_vma=False
    )
```
